256 devices in a mesh: replica: 16 (over y_lo, z), shard: 16 (over y_hi, x, core).
Axes of the slice: x: 4, y: 4 (y_hi: 2, y_lo: 2; y = y_hi * 2 + y_lo), z: 8, core: 2. Of those that a mesh axis runs over, the one named last changes fastest.
Arguments:
- grads: bfloat16 [16, 3072, 8192], P('replica', 'shard'), may hold values from -6 to 6
- errors: bfloat16 [16, 3072, 8192], P('replica', 'shard'), may hold values from -4 to 4
- basis: bfloat16 [3072, 512], P('shard'), may hold values from -0.109375 to 0.109375
- params: float32 [3072, 8192], P('replica', 'shard'), may hold values from -6 to 6
- momentum: float32 [3072, 8192], P('replica', 'shard'), may hold values from -1.2 to 1.2
Outputs:
- new_params: float32 [3072, 8192], P('replica', 'shard')
- new_momentum: float32 [3072, 8192], P('replica', 'shard')
- new_errors: bfloat16 [16, 3072, 8192], P('replica', 'shard')
The draws below stay inside these ranges and needn't reach their ends.
All inputs are finite; a program needn't handle non-finite values.
Results may differ from the reference program's by a relative error of at most 0.012.
Values may be sent and summed in bfloat16 or wider, within the bound.
A program may use at most 128 MiB of HBM per device.

```python
import jax
import jax.numpy as jnp
from jax import lax

ROWS = 3072
COLS = 8192
RANK = 512
REPLICAS = 16
N_REPLICA = 16
N_SHARD = 16


def block_scale(stream_key, dims, shards, smallest, high):
    level = 1.0
    for dim, shards_of in shards:
        draws = jax.random.uniform(jax.random.fold_in(jax.random.fold_in(stream_key, 6), dim), (shards_of,), jnp.float32, smallest / len(shards), high / len(shards))
        level = level * jnp.repeat(jnp.exp(draws), dims[dim] // shards_of).reshape((-1,) + (1,) * (len(dims) - 1 - dim))
    return level


def scatter_about(own_key, extent, width, bound, split=(), dtype=jnp.bfloat16):
    factor_of = block_scale(own_key, extent, split, -0.22, 0.18) if split else 1.0
    values = jax.random.normal(own_key, extent, jnp.float32) * width * factor_of
    return jnp.minimum(jnp.maximum(values, -bound), bound).astype(dtype)


def setup_inputs(seed: int = 0) -> dict:
    streams_of = jax.random.split(jax.random.key(seed), 6)
    return {
        "grads": scatter_about(streams_of[0], (REPLICAS, ROWS, COLS), 1.0, 6.0, ((0, 16), (1, 16))),
        "errors": scatter_about(streams_of[1], (REPLICAS, ROWS, COLS), 0.5, 4.0, ((0, 16), (1, 16))),
        "basis": scatter_about(streams_of[2], (ROWS, RANK), ROWS ** -0.5, 0.109375, ((0, 16),)),
        "params": scatter_about(streams_of[3], (ROWS, COLS), 1.0, 6.0, ((0, 16), (1, 16)), jnp.float32),
        "momentum": scatter_about(streams_of[4], (ROWS, COLS), 0.2, 1.2, ((0, 16), (1, 16)), jnp.float32),
    }


momentum_rate = 0.9
outer_rate = 0.7


def reference(grads, errors, basis, params, momentum):
    rows_dev = ROWS // N_SHARD

    def one_replica(pair):
        grad_block, error_block = pair
        corrected = (grad_block.astype(jnp.float32) + error_block.astype(jnp.float32)).astype(jnp.bfloat16)

        def add_shard(shard_number, running):
            offset = (shard_number * rows_dev).astype(jnp.int32)
            row_block = lax.dynamic_slice_in_dim(corrected, offset, rows_dev, 0)
            basis_block = lax.dynamic_slice_in_dim(basis, offset, rows_dev, 0)
            partial_value = jnp.dot(row_block.T, basis_block, preferred_element_type=jnp.float32)
            rounded = lax.optimization_barrier(partial_value.astype(jnp.bfloat16))
            return running + rounded.astype(jnp.float32)

        running = lax.fori_loop(0, N_SHARD, add_shard, jnp.zeros((COLS, RANK), jnp.float32))
        coeff = running.astype(jnp.bfloat16)
        rebuilt = jnp.dot(basis, coeff.T, preferred_element_type=jnp.float32)
        new_error = (corrected.astype(jnp.float32) - rebuilt).astype(jnp.bfloat16)
        return new_error, coeff

    new_errors, coeffs = lax.map(one_replica, (grads, errors))
    mean_coeff = (jnp.sum(coeffs.astype(jnp.float32), axis=0) * (1.0 / N_REPLICA)).astype(jnp.bfloat16)
    outer_grad = jnp.dot(basis, mean_coeff.T, preferred_element_type=jnp.float32)
    new_momentum = momentum_rate * momentum + outer_grad
    new_params = params - outer_rate * (outer_grad + momentum_rate * new_momentum)
    return new_params, new_momentum, new_errors
```

```python
import jax
import jax.numpy as jnp
from jax import lax
from jax.experimental import pallas as pl
from jax.experimental.pallas import tpu as pltpu
from jax.sharding import PartitionSpec as P

momentum_rate = 0.9
outer_rate = 0.7
MESH = pl.DeviceIdType.MESH
F32, BF16 = jnp.float32, jnp.bfloat16

Y_FIRST = (True, True)
STAGES = 2
ROWS, RANK, LANES = 192, 512, 128


def kernel(g, e, b, o, og, ge, sb, cb, bb, bt, ps, kp, pr, xs, xr, cf, er, rep, rz, ys, yr, mean, bown,
           ldsem, bsem_s, bsem_r, s1, r1, s2, r2, s3, r3, s5, r5, s6, r6, zs, zr, ysm, yrm, as_, ar, osem, lsem):
    shard, replica = lax.axis_index("shard"), lax.axis_index("replica")
    yh, x, c = shard // 8, lax.rem(shard // 2, 4), lax.rem(shard, 2)
    yl, z = replica // 8, lax.rem(replica, 8)
    par = lax.rem(x, 2)
    na = x + 1 - 2 * par
    nb = lax.rem(x + 3 + 2 * par, 4)

    def at(yh_=None, x_=None, c_=None, yl_=None, z_=None):
        yh_ = yh if yh_ is None else yh_
        x_ = x if x_ is None else x_
        c_ = c if c_ is None else c_
        yl_ = yl if yl_ is None else yl_
        z_ = z if z_ is None else z_
        return (yl_ * 8 + z_, (yh_ * 4 + x_) * 2 + c_)

    def remote(src, dst, ss, rs, dev):
        return pltpu.make_async_remote_copy(
            src_ref=src, dst_ref=dst, send_sem=ss, recv_sem=rs, device_id=dev, device_id_type=MESH)

    def nd(h):
        return na + h * (nb - na)

    def xp(h):
        return nb + h * (na - nb)

    def member(h, m):
        return at(x_=x if m < 2 else nd(h), c_=c if m % 2 == 0 else 1 - c)

    def pos(h, m):
        return lax.rem(m + 2 * (1 - h), 4)

    def rows_of(h, m):
        return pl.ds(pl.multiple_of(pos(h, m) * ROWS, ROWS), ROWS)

    def my_maj(k, m=0):
        if Y_FIRST[k]:
            return yh
        return par if m < 2 else 1 - par

    def my_min(k):
        return par if Y_FIRST[k] else yh

    def column(k, h, m, maj, mn):
        x_d = x if m < 2 else nd(h)
        x_p = xp(h) if m < 2 else lax.rem(x + 2, 4)
        c_d = c if m % 2 == 0 else 1 - c
        y_o, q = (maj, mn) if Y_FIRST[k] else (mn, maj)
        x_o = x_d + (x_p - x_d) * lax.rem(lax.rem(x_d, 2) + q, 2)
        start = ((y_o * 4 + x_o) * 2 + c_d) * 512 + h * 256 + k * LANES
        return pl.ds(pl.multiple_of(start, LANES), LANES)

    def p1(k, h):
        return at(yh_=1 - yh) if Y_FIRST[k] else at(x_=xp(h))

    def p2(k, h):
        return at(x_=xp(h)) if Y_FIRST[k] else at(yh_=1 - yh)

    def halves(body):
        def step(h, carry):
            body(h)
            return carry
        lax.fori_loop(0, 2, step, 0)

    barrier = pltpu.get_barrier_semaphore()
    partners = [at(c_=1 - c), at(x_=na), at(x_=na, c_=1 - c), at(x_=nb), at(x_=nb, c_=1 - c), at(yh_=1 - yh),
                at(yl_=1 - yl)] + [at(z_=lax.rem(z + d, 8)) for d in range(1, 8)]
    for p in partners:
        pl.semaphore_signal(barrier, inc=1, device_id=p, device_id_type=MESH)
    off_diagonal = shard != replica

    @pl.when(off_diagonal)
    def _():
        pl.semaphore_signal(barrier, inc=1, device_id=(shard, replica), device_id_type=MESH)

    own_b = pltpu.make_async_copy(b, bb.at[pl.ds(2 * ROWS, ROWS)], lsem.at[0])
    own_b.start()
    order = (2, 3, 1, 0)

    def maj_of(k, m, s):
        return lax.rem(my_maj(k, m) + 1 + s, 2)

    def load(k, s):
        for m in order:
            def one(h):
                maj = maj_of(k, m, s)
                for mn in range(2):
                    cols = column(k, h, m, maj, mn)
                    for w, src in enumerate((g, e)):
                        pltpu.make_async_copy(
                            src.at[0, :, cols], ge.at[k, h, m, maj, w, :, pl.ds(mn * LANES, LANES)],
                            ldsem.at[k, h, m, maj]).start()
            halves(one)

    def correct(k, s):
        for m in order:
            def one(h):
                maj = maj_of(k, m, s)
                piece = ge.at[k, h, m, maj]
                pltpu.make_async_copy(piece, piece, ldsem.at[k, h, m, maj]).wait()
                val = (ge[k, h, m, maj, 0].astype(F32) + ge[k, h, m, maj, 1].astype(F32)).astype(BF16)
                if m == 0:
                    cb[k, h, maj, rows_of(h, 0), :] = val
                else:
                    sb[k, h, m - 1, maj] = val
                    send1(k, h, m, maj).start()
            halves(one)

    def send1(k, h, m, maj):
        return remote(sb.at[k, h, m - 1, maj], cb.at[k, h, maj, rows_of(h, m)],
                      s1.at[k, h, m - 1, maj], r1.at[k, h, m - 1, maj], member(h, m))

    for k in range(STAGES):
        for s in range(2):
            load(k, s)

    pl.semaphore_wait(barrier, len(partners) + jnp.where(off_diagonal, 1, 0))

    def slot(i):
        return bb.at[pl.ds(i * ROWS, ROWS)]

    own_b.wait()
    basis_sends = [
        remote(slot(2), slot(0), bsem_s.at[0], bsem_r.at[0], at(x_=na)),
        remote(slot(2), slot(4), bsem_s.at[1], bsem_r.at[1], at(x_=nb)),
        remote(slot(2), slot(3), bsem_s.at[2], bsem_r.at[2], at(c_=1 - c)),
        remote(slot(0), slot(1), bsem_s.at[3], bsem_r.at[3], at(c_=1 - c)),
        remote(slot(4), slot(5), bsem_s.at[4], bsem_r.at[4], at(c_=1 - c)),
    ]
    for cp in basis_sends[:3]:
        cp.start()

    correct(0, 0)
    correct(1, 0)
    for i in range(2):
        basis_sends[i].wait_recv()
        basis_sends[3 + i].start()
    correct(0, 1)
    correct(1, 1)

    own_rows = remote(slot(2), bown, bsem_s.at[5], bsem_r.at[5], (shard, replica))
    own_rows_here = pltpu.make_async_copy(slot(2), bown, lsem.at[1])

    @pl.when(off_diagonal)
    def _():
        own_rows.start()

    @pl.when(shard == replica)
    def _():
        own_rows_here.start()

    for i in range(2, 5):
        basis_sends[i].wait_recv()

    def turn(i, carry):
        bt[:, pl.ds(pl.multiple_of(i * 2 * ROWS, 128), 2 * ROWS)] = bb[pl.ds(pl.multiple_of(i * 2 * ROWS, 128), 2 * ROWS), :].T
        return carry
    lax.fori_loop(0, 3, turn, 0)

    def send2(k, h):
        return remote(ps.at[k, h], pr.at[k, h], s2.at[k, h], r2.at[k, h], p1(k, h))

    def partial(k, s):
        def one(h):
            maj = maj_of(k, 0, s)
            for m in range(1, 4):
                send1(k, h, m, maj).wait_recv()

            def tile(i, carry):
                rk = pl.ds(pl.multiple_of(i * 256, 256), 256)
                val = jnp.dot(bt[rk, pl.ds(pl.multiple_of(h * 2 * ROWS, 128), 4 * ROWS)], cb[k, h, maj],
                              preferred_element_type=F32)
                if s == 0:
                    ps[k, h, rk, :] = val.astype(BF16)
                else:
                    kp[k, h, rk, :] = val
                return carry
            lax.fori_loop(0, 2, tile, 0)
            if s == 0:
                send2(k, h).start()
        halves(one)

    def send3(k, h):
        return remote(xs.at[k, h], xr.at[k, h], s3.at[k, h], r3.at[k, h], p2(k, h))

    def exchange(k):
        def one(h):
            send2(k, h).wait_recv()
            xs[k, h] = (kp[k, h] + pr[k, h].astype(F32)).astype(BF16)
            send3(k, h).start()
        halves(one)

    def send5(k, h):
        return remote(cf.at[k, h, my_maj(k)], cf.at[k, h, my_maj(k)], s5.at[k, h], r5.at[k, h], p1(k, h))

    def zsend(k, d):
        to = lax.rem(z + d, 8)
        return remote(rep.at[k, to], rz.at[k, d], zs.at[k, d], zr.at[k, d], at(z_=to))

    def coefficients(k):
        def one(h):
            send3(k, h).wait_recv()
            cf[k, h, my_maj(k)] = (xs[k, h].astype(F32) + xr[k, h].astype(F32)).astype(BF16)
            send5(k, h).start()
            mine = cf[k, h, my_maj(k), :, pl.ds(pl.multiple_of(my_min(k) * LANES, LANES), LANES)]
            rep[k, :, h] = mine.reshape(8, 64, LANES)
        halves(one)
        for d in range(1, 8):
            zsend(k, d).start()

    def send6(k, h, m, maj, mn):
        src = er.at[k, h, maj, rows_of(h, m), pl.ds(mn * LANES, LANES)]
        dst = o.at[0, :, column(k, h, 0, maj, mn)]
        return remote(src, dst, s6.at[k, h, m - 1, maj, mn], r6.at[k, h, m - 1, maj, mn], member(h, m))

    def keep6(k, h, maj, mn):
        src = er.at[k, h, maj, rows_of(h, 0), pl.ds(mn * LANES, LANES)]
        return pltpu.make_async_copy(src, o.at[0, :, column(k, h, 0, maj, mn)], osem.at[k, h, maj, mn])

    def receive6(k, h, m, maj, mn):
        src = er.at[k, h, maj, rows_of(h, m), pl.ds(mn * LANES, LANES)]
        dst = o.at[0, :, column(k, h, m, maj, mn)]
        return remote(src, dst, s6.at[k, h, m - 1, maj, mn], r6.at[k, h, m - 1, maj, mn], member(h, m))

    def rebuild(k, s):
        def one(h):
            maj = lax.rem(my_maj(k) + s, 2)
            if s == 1:
                send5_other(k, h).wait_recv()
            for pair in range(2):
                off = h * 2 * ROWS if pair == 0 else (1 - h) * 2 * ROWS
                off = pl.multiple_of(off, 128)
                both = pl.ds(off, 2 * ROWS)
                val = jnp.dot(bb[pl.ds(pl.multiple_of(h * 2 * ROWS + off, 128), 2 * ROWS), :], cf[k, h, maj],
                              preferred_element_type=F32)
                er[k, h, maj, both, :] = (cb[k, h, maj, both, :].astype(F32) - val).astype(BF16)
                for mn in range(2):
                    if pair == 0:
                        send6(k, h, 2, maj, mn).start()
                        send6(k, h, 3, maj, mn).start()
                    else:
                        send6(k, h, 1, maj, mn).start()
                        keep6(k, h, maj, mn).start()
        halves(one)

    def send5_other(k, h):
        other = 1 - my_maj(k)
        return remote(cf.at[k, h, other], cf.at[k, h, other], s5.at[k, h], r5.at[k, h], p1(k, h))

    def ysend(k):
        return remote(ys.at[k], yr.at[k], ysm.at[k], yrm.at[k], at(yl_=1 - yl))

    def z_total(k):
        total = rep[k, z].astype(F32)
        for d in range(1, 8):
            zsend(k, d).wait_recv()
            total = total + rz[k, d].astype(F32)
        ys[k] = total
        ysend(k).start()

    def asend(k, d):
        return remote(mean.at[k, z], mean.at[k, z], as_.at[k, d], ar.at[k, d], at(z_=lax.rem(z + d, 8)))

    def arecv(k, d):
        frm = lax.rem(z - d + 8, 8)
        return remote(mean.at[k, frm], mean.at[k, frm], as_.at[k, d], ar.at[k, d], at(z_=lax.rem(z + d, 8)))

    def z_mean(k):
        ysend(k).wait_recv()
        mean[k, z] = ((ys[k] + yr[k]) * (1.0 / 16.0)).astype(BF16)
        for d in range(1, 8):
            asend(k, d).start()

    def outer(k):
        for d in range(1, 8):
            arecv(k, d).wait_recv()
        for h in range(2):
            lanes = pl.ds(h * 256 + k * LANES, LANES)
            og[:, lanes] = jnp.dot(bown[...], mean[k, :, h].reshape(RANK, LANES), preferred_element_type=F32)

    partial(0, 0)
    partial(1, 0)
    partial(0, 1)
    exchange(0)
    partial(1, 1)
    coefficients(0)
    rebuild(0, 0)
    exchange(1)
    z_total(0)
    coefficients(1)
    rebuild(1, 0)
    z_mean(0)
    rebuild(0, 1)
    z_total(1)

    @pl.when(off_diagonal)
    def _():
        own_rows.wait_recv()

    @pl.when(shard == replica)
    def _():
        own_rows_here.wait()

    outer(0)
    z_mean(1)
    rebuild(1, 1)
    outer(1)

    for cp in basis_sends:
        cp.wait_send()

    @pl.when(off_diagonal)
    def _():
        own_rows.wait_send()

    for k in range(STAGES):
        def one(h):
            for maj in range(2):
                for m in range(1, 4):
                    send1(k, h, m, maj).wait_send()
                    for mn in range(2):
                        send6(k, h, m, maj, mn).wait_send()
                        receive6(k, h, m, maj, mn).wait_recv()
                for mn in range(2):
                    keep6(k, h, maj, mn).wait()
            send2(k, h).wait_send()
            send3(k, h).wait_send()
            send5(k, h).wait_send()
        halves(one)
        for d in range(1, 8):
            zsend(k, d).wait_send()
            asend(k, d).wait_send()
        ysend(k).wait_send()


def exchange_step(grads, errors, basis):
    K = STAGES
    any_, vmem = pl.BlockSpec(memory_space=pl.ANY), pl.BlockSpec(memory_space=pltpu.VMEM)
    hbm = pl.BlockSpec(memory_space=pltpu.HBM)
    D = pltpu.SemaphoreType.DMA
    V = pltpu.VMEM
    return pl.pallas_call(
        kernel,
        out_shape=(jax.ShapeDtypeStruct(grads.shape, BF16), jax.ShapeDtypeStruct((ROWS, 512), F32)),
        in_specs=[hbm, hbm, hbm],
        out_specs=(any_, vmem),
        scratch_shapes=[
            V((K, 2, 4, 2, 2, ROWS, 256), BF16),
            V((K, 2, 3, 2, ROWS, 256), BF16),
            V((K, 2, 2, 4 * ROWS, 256), BF16),
            V((6 * ROWS, RANK), BF16),
            V((RANK, 6 * ROWS), BF16),
            V((K, 2, RANK, 256), BF16),
            V((K, 2, RANK, 256), F32),
            V((K, 2, RANK, 256), BF16),
            V((K, 2, RANK, 256), BF16),
            V((K, 2, RANK, 256), BF16),
            V((K, 2, 2, RANK, 256), BF16),
            V((K, 2, 2, 4 * ROWS, 256), BF16),
            V((K, 8, 2, 64, LANES), BF16),
            V((K, 8, 2, 64, LANES), BF16),
            V((K, 2, 64, LANES), F32),
            V((K, 2, 64, LANES), F32),
            V((K, 8, 2, 64, LANES), BF16),
            V((ROWS, RANK), BF16),
            D((K, 2, 4, 2)),
            D((6,)), D((6,)),
            D((K, 2, 3, 2)), D((K, 2, 3, 2)),
            D((K, 2)), D((K, 2)),
            D((K, 2)), D((K, 2)),
            D((K, 2)), D((K, 2)),
            D((K, 2, 3, 2, 2)), D((K, 2, 3, 2, 2)),
            D((K, 8)), D((K, 8)),
            D((K,)), D((K,)),
            D((K, 8)), D((K, 8)),
            D((K, 2, 2, 2)),
            D((2,)),
        ],
        compiler_params=pltpu.CompilerParams(
            collective_id=0, has_side_effects=True, vmem_limit_bytes=40 << 20),
        name="exchange_step",
    )(*(pltpu.with_memory_space_constraint(a, pltpu.HBM) for a in (grads, errors, basis)))


def body(grads, errors, basis, params, momentum):
    new_error, outer_grad = exchange_step(grads, errors, basis)
    new_momentum = momentum_rate * momentum + outer_grad
    new_params = params - outer_rate * (outer_grad + momentum_rate * new_momentum)
    return (new_params, new_momentum, new_error)


def solution(mesh):
    in_specs = (
        P("replica", "shard", None),
        P("replica", "shard", None),
        P("shard", None),
        P("replica", "shard"),
        P("replica", "shard"),
    )
    out_specs = (P("replica", "shard"), P("replica", "shard"), P("replica", "shard", None))
    return jax.shard_map(body, mesh=mesh, in_specs=in_specs, out_specs=out_specs, check_vma=False)
```

```python
import jax
import jax.numpy as jnp
from jax import lax
from jax.experimental import pallas as pl
from jax.experimental.pallas import tpu as pltpu
from jax.sharding import PartitionSpec as P

momentum_rate = 0.9
outer_rate = 0.7
MESH = pl.DeviceIdType.MESH
F32, BF16 = jnp.float32, jnp.bfloat16

Y_FIRST = (True, True)
STAGES = 2
ROWS, RANK, LANES = 192, 512, 128
SCHEDULE = (
    ("basis_start",),
    ("correct", 0, 0),
    ("own_start",),
    ("basis_pass", 0),
    ("correct", 1, 0),
    ("basis_pass", 1),
    ("correct", 0, 1),
    ("basis_pass", 2),
    ("partial", 0, 0),
    ("correct", 1, 1),
    ("partial", 1, 0),
    ("partial", 0, 1),
    ("exchange", 0),
    ("partial", 1, 1),
    ("coefficients", 0),
    ("rebuild", 0, 0),
    ("exchange", 1),
    ("z_total", 0),
    ("coefficients", 1),
    ("rebuild", 1, 0),
    ("z_mean", 0),
    ("rebuild", 0, 1),
    ("z_total", 1),
    ("own_wait",),
    ("outer", 0),
    ("z_mean", 1),
    ("rebuild", 1, 1),
    ("outer", 1),
)


def kernel(g, e, b, o, og, gb, eb, sb, cb, bb, bt, ps, kp, pr, xs, xr, cf, er, rep, rz, ys, yr, mean, bown,
           ldsem, bsem_s, bsem_r, s1, r1, s2, r2, s3, r3, s5, r5, s6, r6, zs, zr, ysm, yrm, as_, ar, osem, lsem):
    shard, replica = lax.axis_index("shard"), lax.axis_index("replica")
    yh, x, c = shard // 8, lax.rem(shard // 2, 4), lax.rem(shard, 2)
    yl, z = replica // 8, lax.rem(replica, 8)
    par = lax.rem(x, 2)
    na = x + 1 - 2 * par
    nb = lax.rem(x + 3 + 2 * par, 4)

    def at(yh_=None, x_=None, c_=None, yl_=None, z_=None):
        yh_ = yh if yh_ is None else yh_
        x_ = x if x_ is None else x_
        c_ = c if c_ is None else c_
        yl_ = yl if yl_ is None else yl_
        z_ = z if z_ is None else z_
        return (yl_ * 8 + z_, (yh_ * 4 + x_) * 2 + c_)

    def remote(src, dst, ss, rs, dev):
        return pltpu.make_async_remote_copy(
            src_ref=src, dst_ref=dst, send_sem=ss, recv_sem=rs, device_id=dev, device_id_type=MESH)

    def nd(h):
        return na + h * (nb - na)

    def xp(h):
        return nb + h * (na - nb)

    def member(h, m):
        return at(x_=x if m < 2 else nd(h), c_=c if m % 2 == 0 else 1 - c)

    def pos(h, m):
        return lax.rem(m + 2 * (1 - h), 4)

    def rows_of(h, m):
        return pl.ds(pl.multiple_of(pos(h, m) * ROWS, ROWS), ROWS)

    def my_maj(k, m=0):
        if Y_FIRST[k]:
            return yh
        return par if m < 2 else 1 - par

    def my_min(k):
        return par if Y_FIRST[k] else yh

    def column(k, h, m, maj, mn):
        x_d = x if m < 2 else nd(h)
        x_p = xp(h) if m < 2 else lax.rem(x + 2, 4)
        c_d = c if m % 2 == 0 else 1 - c
        y_o, q = (maj, mn) if Y_FIRST[k] else (mn, maj)
        x_o = x_d + (x_p - x_d) * lax.rem(lax.rem(x_d, 2) + q, 2)
        start = ((y_o * 4 + x_o) * 2 + c_d) * 512 + h * 256 + k * LANES
        return pl.ds(pl.multiple_of(start, LANES), LANES)

    def p1(k, h):
        return at(yh_=1 - yh) if Y_FIRST[k] else at(x_=xp(h))

    def p2(k, h):
        return at(x_=xp(h)) if Y_FIRST[k] else at(yh_=1 - yh)

    def halves(body):
        def step(h, carry):
            body(h)
            return carry
        lax.fori_loop(0, 2, step, 0)

    own_b = pltpu.make_async_copy(b, bb.at[pl.ds(2 * ROWS, ROWS)], lsem.at[0])
    own_b.start()
    loads = [
        pltpu.make_async_copy(src.at[0, pl.ds(i * 96, 96)], dst.at[pl.ds(i * 96, 96)], ldsem.at[2 * w + i])
        for i in range(2) for w, (src, dst) in enumerate(((g, gb), (e, eb)))
    ]
    for cp in loads:
        cp.start()

    barrier = pltpu.get_barrier_semaphore()
    partners = [at(c_=1 - c), at(x_=na), at(x_=na, c_=1 - c), at(x_=nb), at(x_=nb, c_=1 - c), at(yh_=1 - yh),
                at(yl_=1 - yl)] + [at(z_=lax.rem(z + d, 8)) for d in range(1, 8)]
    for p in partners:
        pl.semaphore_signal(barrier, inc=1, device_id=p, device_id_type=MESH)
    off_diagonal = shard != replica

    @pl.when(off_diagonal)
    def _():
        pl.semaphore_signal(barrier, inc=1, device_id=(shard, replica), device_id_type=MESH)

    order = (2, 3, 1, 0)

    def maj_of(k, m, s):
        return lax.rem(my_maj(k, m) + 1 + s, 2)

    def correct(k, s):
        for m in order:
            def one(h):
                maj = maj_of(k, m, s)
                for mn in range(2):
                    cols = column(k, h, m, maj, mn)
                    lanes = pl.ds(mn * LANES, LANES)
                    val = (gb[:, cols].astype(F32) + eb[:, cols].astype(F32)).astype(BF16)
                    if m == 0:
                        cb[k, h, maj, rows_of(h, 0), lanes] = val
                    else:
                        sb[k, h, m - 1, maj, :, lanes] = val
                if m:
                    send1(k, h, m, maj).start()
            halves(one)

    def send1(k, h, m, maj):
        return remote(sb.at[k, h, m - 1, maj], cb.at[k, h, maj, rows_of(h, m)], s1.at[0], r1.at[k, h, maj], member(h, m))

    def done(sem, like):
        return pltpu.make_async_copy(like, like, sem)

    pl.semaphore_wait(barrier, len(partners) + jnp.where(off_diagonal, 1, 0))

    def slot(i):
        return bb.at[pl.ds(i * ROWS, ROWS)]

    half = pl.ds(pl.multiple_of(lax.rem(z, 2) * 96, 96), 96)
    rest = pl.ds(pl.multiple_of((1 - lax.rem(z, 2)) * 96, 96), 96)
    zp = at(z_=z + 1 - 2 * lax.rem(z, 2))

    def basis_copy(i, src, dst, dev):
        return remote(src, dst, bsem_s.at[i], bsem_r.at[i], dev)

    own_b.wait()
    basis_copies = []
    for i, (near, far, dev) in enumerate(((0, 1, at(x_=na)), (4, 5, at(x_=nb)))):
        mine = slot(2).at[half]
        basis_copies += [
            basis_copy(6 * i, mine, slot(near).at[half], dev),
            basis_copy(6 * i + 1, slot(near).at[half], slot(near).at[half], zp),
            basis_copy(6 * i + 2, slot(near).at[half], slot(far).at[half], at(c_=1 - c)),
            basis_copy(6 * i + 3, slot(near).at[rest], slot(far).at[rest], at(c_=1 - c)),
        ]
    basis_core = basis_copy(4, slot(2), slot(3), at(c_=1 - c))

    def basis_from_z(i):
        near = (0, 4)[i]
        return basis_copy(6 * i + 1, slot(near).at[half], slot(near).at[rest], zp)

    def basis_start():
        basis_copies[0].start()
        basis_copies[4].start()
        basis_core.start()

    def basis_pass(step):
        for i in range(2):
            if step == 0:
                basis_copies[4 * i].wait_recv()
                basis_copies[4 * i + 1].start()
                basis_copies[4 * i + 2].start()
            elif step == 1:
                basis_from_z(i).wait_recv()
                basis_copies[4 * i + 3].start()
            else:
                basis_copies[4 * i + 2].wait_recv()
                basis_copies[4 * i + 3].wait_recv()
        if step == 2:
            basis_core.wait_recv()

            def turn(i, carry):
                at_ = pl.ds(pl.multiple_of(i * 2 * ROWS, 128), 2 * ROWS)
                bt[:, at_] = bb[at_, :].T
                return carry
            lax.fori_loop(0, 3, turn, 0)

    own_rows = remote(slot(2), bown, bsem_s.at[5], bsem_r.at[5], (shard, replica))
    own_rows_here = pltpu.make_async_copy(slot(2), bown, lsem.at[1])

    def own_start():
        @pl.when(off_diagonal)
        def _():
            own_rows.start()

        @pl.when(shard == replica)
        def _():
            own_rows_here.start()

    def own_wait():
        @pl.when(off_diagonal)
        def _():
            own_rows.wait_recv()

        @pl.when(shard == replica)
        def _():
            own_rows_here.wait()

    def send2(k, h):
        return remote(ps.at[k, h], pr.at[k, h], s2.at[0], r2.at[k, h], p1(k, h))

    def partial(k, s):
        def one(h):
            maj = maj_of(k, 0, s)
            done(r1.at[k, h, maj], cb.at[k, h, maj, pl.ds(0, 3 * ROWS)]).wait()

            def tile(i, carry):
                rk = pl.ds(pl.multiple_of(i * 256, 256), 256)
                val = jnp.dot(bt[rk, pl.ds(pl.multiple_of(h * 2 * ROWS, 128), 4 * ROWS)], cb[k, h, maj],
                              preferred_element_type=F32)
                if s == 0:
                    ps[k, h, rk, :] = val.astype(BF16)
                else:
                    kp[k, h, rk, :] = val
                return carry
            lax.fori_loop(0, 2, tile, 0)
            if s == 0:
                send2(k, h).start()
        halves(one)

    def send3(k, h):
        return remote(xs.at[k, h], xr.at[k, h], s3.at[0], r3.at[k, h], p2(k, h))

    def exchange(k):
        def one(h):
            send2(k, h).wait_recv()
            xs[k, h] = (kp[k, h] + pr[k, h].astype(F32)).astype(BF16)
            send3(k, h).start()
        halves(one)

    def send5(k, h):
        return remote(cf.at[k, h, my_maj(k)], cf.at[k, h, my_maj(k)], s5.at[0], r5.at[k, h], p1(k, h))

    def zsend(k, d):
        to = lax.rem(z + d, 8)
        return remote(rep.at[k, to], rz.at[k, d], zs.at[0], zr.at[k], at(z_=to))

    def coefficients(k):
        def one(h):
            send3(k, h).wait_recv()
            cf[k, h, my_maj(k)] = (xs[k, h].astype(F32) + xr[k, h].astype(F32)).astype(BF16)
            send5(k, h).start()
            mine = cf[k, h, my_maj(k), :, pl.ds(pl.multiple_of(my_min(k) * LANES, LANES), LANES)]
            rep[k, :, h] = mine.reshape(8, 64, LANES)
        halves(one)
        for d in range(1, 8):
            zsend(k, d).start()

    def send6(k, h, m, maj, mn):
        src = er.at[k, h, maj, rows_of(h, m), pl.ds(mn * LANES, LANES)]
        dst = o.at[0, :, column(k, h, 0, maj, mn)]
        return remote(src, dst, s6.at[0], r6.at[0], member(h, m))

    def keep6(k, h, maj, mn):
        src = er.at[k, h, maj, rows_of(h, 0), pl.ds(mn * LANES, LANES)]
        return pltpu.make_async_copy(src, o.at[0, :, column(k, h, 0, maj, mn)], osem.at[0])

    def rebuild(k, s):
        def one(h):
            maj = lax.rem(my_maj(k) + s, 2)
            if s == 1:
                send5_other(k, h).wait_recv()
            for pair in range(2):
                off = h * 2 * ROWS if pair == 0 else (1 - h) * 2 * ROWS
                off = pl.multiple_of(off, 128)
                both = pl.ds(off, 2 * ROWS)
                val = jnp.dot(bb[pl.ds(pl.multiple_of(h * 2 * ROWS + off, 128), 2 * ROWS), :], cf[k, h, maj],
                              preferred_element_type=F32)
                er[k, h, maj, both, :] = (cb[k, h, maj, both, :].astype(F32) - val).astype(BF16)
                for mn in range(2):
                    if pair == 0:
                        send6(k, h, 2, maj, mn).start()
                        send6(k, h, 3, maj, mn).start()
                    else:
                        send6(k, h, 1, maj, mn).start()
                        keep6(k, h, maj, mn).start()
        halves(one)

    def send5_other(k, h):
        other = 1 - my_maj(k)
        return remote(cf.at[k, h, other], cf.at[k, h, other], s5.at[0], r5.at[k, h], p1(k, h))

    def ysend(k):
        return remote(ys.at[k], yr.at[k], ysm.at[k], yrm.at[k], at(yl_=1 - yl))

    def z_total(k):
        total = rep[k, z].astype(F32)
        done(zr.at[k], rz.at[k, pl.ds(1, 7)]).wait()
        for d in range(1, 8):
            total = total + rz[k, d].astype(F32)
        ys[k] = total
        ysend(k).start()

    def asend(k, d):
        return remote(mean.at[k, z], mean.at[k, z], as_.at[0], ar.at[k], at(z_=lax.rem(z + d, 8)))

    def z_mean(k):
        ysend(k).wait_recv()
        mean[k, z] = ((ys[k] + yr[k]) * (1.0 / 16.0)).astype(BF16)
        for d in range(1, 8):
            asend(k, d).start()

    def outer(k):
        done(ar.at[k], rz.at[k, pl.ds(1, 7)]).wait()
        for h in range(2):
            lanes = pl.ds(h * 256 + k * LANES, LANES)
            og[:, lanes] = jnp.dot(bown[...], mean[k, :, h].reshape(RANK, LANES), preferred_element_type=F32)

    for cp in loads:
        cp.wait()
    events = dict(basis_start=basis_start, basis_pass=basis_pass, own_start=own_start, own_wait=own_wait, correct=correct,
                  partial=partial, exchange=exchange, coefficients=coefficients, rebuild=rebuild, z_total=z_total,
                  z_mean=z_mean, outer=outer)
    for name, *where in SCHEDULE:
        events[name](*where)

    for cp in basis_copies + [basis_core]:
        cp.wait_send()

    @pl.when(off_diagonal)
    def _():
        own_rows.wait_send()

    done(s1.at[0], sb).wait()
    done(s2.at[0], ps).wait()
    done(s3.at[0], xs).wait()
    done(s5.at[0], pr).wait()
    for k in range(STAGES):
        ysend(k).wait_send()
    done(zs.at[0], rz.at[:, pl.ds(1, 7)]).wait()
    done(as_.at[0], rz.at[:, pl.ds(1, 7)]).wait()
    done(osem.at[0], er.at[:, :, :, pl.ds(0, ROWS)]).wait()
    done(s6.at[0], sb).wait()
    done(r6.at[0], sb).wait()


def exchange_step(grads, errors, basis):
    K = STAGES
    any_, vmem = pl.BlockSpec(memory_space=pl.ANY), pl.BlockSpec(memory_space=pltpu.VMEM)
    hbm = pl.BlockSpec(memory_space=pltpu.HBM)
    D = pltpu.SemaphoreType.DMA
    V = pltpu.VMEM
    return pl.pallas_call(
        kernel,
        out_shape=(jax.ShapeDtypeStruct(grads.shape, BF16), jax.ShapeDtypeStruct((ROWS, 512), F32)),
        in_specs=[hbm, hbm, hbm],
        out_specs=(any_, vmem),
        scratch_shapes=[
            V((ROWS, 8192), BF16),
            V((ROWS, 8192), BF16),
            V((K, 2, 3, 2, ROWS, 256), BF16),
            V((K, 2, 2, 4 * ROWS, 256), BF16),
            V((6 * ROWS, RANK), BF16),
            V((RANK, 6 * ROWS), BF16),
            V((K, 2, RANK, 256), BF16),
            V((K, 2, RANK, 256), F32),
            V((K, 2, RANK, 256), BF16),
            V((K, 2, RANK, 256), BF16),
            V((K, 2, RANK, 256), BF16),
            V((K, 2, 2, RANK, 256), BF16),
            V((K, 2, 2, 4 * ROWS, 256), BF16),
            V((K, 8, 2, 64, LANES), BF16),
            V((K, 8, 2, 64, LANES), BF16),
            V((K, 2, 64, LANES), F32),
            V((K, 2, 64, LANES), F32),
            V((K, 8, 2, 64, LANES), BF16),
            V((ROWS, RANK), BF16),
            D((4,)),
            D((10,)), D((10,)),
            D((1,)), D((K, 2, 2)),
            D((1,)), D((K, 2)),
            D((1,)), D((K, 2)),
            D((1,)), D((K, 2)),
            D((1,)), D((1,)),
            D((1,)), D((K,)),
            D((K,)), D((K,)),
            D((1,)), D((K,)),
            D((1,)),
            D((2,)),
        ],
        compiler_params=pltpu.CompilerParams(
            collective_id=0, has_side_effects=True, vmem_limit_bytes=40 << 20),
        name="exchange_step",
    )(*(pltpu.with_memory_space_constraint(a, pltpu.HBM) for a in (grads, errors, basis)))


def body(grads, errors, basis, params, momentum):
    new_error, outer_grad = exchange_step(grads, errors, basis)
    new_momentum = momentum_rate * momentum + outer_grad
    new_params = params - outer_rate * (outer_grad + momentum_rate * new_momentum)
    return (new_params, new_momentum, new_error)


def solution(mesh):
    in_specs = (
        P("replica", "shard", None),
        P("replica", "shard", None),
        P("shard", None),
        P("replica", "shard"),
        P("replica", "shard"),
    )
    out_specs = (P("replica", "shard"), P("replica", "shard"), P("replica", "shard", None))
    return jax.shard_map(body, mesh=mesh, in_specs=in_specs, out_specs=out_specs, check_vma=False)
```

```python
import jax
import jax.numpy as jnp
from jax import lax
from jax.experimental import pallas as pl
from jax.experimental.pallas import tpu as pltpu
from jax.sharding import PartitionSpec as P

momentum_rate = 0.9
outer_rate = 0.7
MESH = pl.DeviceIdType.MESH
F32, BF16 = jnp.float32, jnp.bfloat16

STAGES = 2
ROWS, RANK, LANES = 192, 512, 128
SCHEDULE = (
    ("basis_start",),
    ("correct", 0, 0),
    ("correct", 1, 0),
    ("correct", 0, 1),
    ("correct", 1, 1),
    ("basis_pass", 0),
    ("basis_pass", 1),
    ("partial", 0, 0),
    ("basis_pass", 2),
    ("partial", 0, 1),
    ("partial", 1, 0),
    ("exchange", 0),
    ("partial", 1, 1),
    ("exchange", 1),
    ("own_start",),
    ("coefficients", 0, 0),
    ("coefficients", 1, 0),
    ("coefficients", 0, 1),
    ("coefficients", 1, 1),
    ("rebuild", 1, 0),
    ("z_total", 0, 0),
    ("rebuild", 0, 0),
    ("z_total", 1, 0),
    ("z_total", 0, 1),
    ("z_total", 1, 1),
    ("rebuild", 1, 1),
    ("z_mean", 0, 0),
    ("z_mean", 1, 0),
    ("z_mean", 0, 1),
    ("z_mean", 1, 1),
    ("rebuild", 0, 1),
    ("own_wait",),
    ("outer", 0, 0),
    ("outer", 1, 0),
    ("outer", 0, 1),
    ("outer", 1, 1),
)


def kernel(g, e, b, o, og, gb, eb, sb, cb, bb, bt, ps, kp, pr, xs, xr, cf, er, rep, rz, ys, yr, mean, bown,
           ldsem, bsem_s, bsem_r, s1, r1, s2, r2, s3, r3, s5, r5, s6, r6, zs, zr, ysm, yrm, as_, ar, osem, lsem):
    shard, replica = lax.axis_index("shard"), lax.axis_index("replica")
    yh, x, c = shard // 8, lax.rem(shard // 2, 4), lax.rem(shard, 2)
    yl, z = replica // 8, lax.rem(replica, 8)
    par = lax.rem(x, 2)
    na = x + 1 - 2 * par
    nb = lax.rem(x + 3 + 2 * par, 4)

    def at(yh_=None, x_=None, c_=None, yl_=None, z_=None):
        yh_ = yh if yh_ is None else yh_
        x_ = x if x_ is None else x_
        c_ = c if c_ is None else c_
        yl_ = yl if yl_ is None else yl_
        z_ = z if z_ is None else z_
        return (yl_ * 8 + z_, (yh_ * 4 + x_) * 2 + c_)

    def remote(src, dst, ss, rs, dev):
        return pltpu.make_async_remote_copy(
            src_ref=src, dst_ref=dst, send_sem=ss, recv_sem=rs, device_id=dev, device_id_type=MESH)

    def near(h):
        return na + h * (nb - na)

    def away(h):
        return nb + h * (na - nb)

    def member(k, h, m):
        c_m = c if m % 2 == 0 else 1 - c
        if m < 2:
            return at(c_=c_m)
        return at(x_=near(h), c_=c_m) if k == 0 else at(yh_=1 - yh, c_=c_m)

    def first_of(k, h, pair):
        if k == 1:
            return pair * 2 * ROWS
        return (h if pair == 0 else 1 - h) * 2 * ROWS

    def basis_row(k, h):
        return h * 2 * ROWS if k == 0 else 6 * ROWS

    def rows_of(k, h, m):
        row = first_of(k, h, 0 if m >= 2 else 1) + (m % 2) * ROWS
        return pl.ds(pl.multiple_of(row, ROWS), ROWS)

    def my_maj(k, h, m=0):
        if k == 0:
            return par if m < 2 else 1 - par
        odd = lax.rem((x + 1) // 2, 2)
        return odd + h * (x // 2 - odd)

    def my_min(k):
        return yh if k == 0 else par

    def column(k, h, m, maj, mn):
        c_d = c if m % 2 == 0 else 1 - c
        if k == 0:
            x_d = x if m < 2 else near(h)
            x_p = away(h) if m < 2 else lax.rem(x + 2, 4)
            y_o = mn
            x_o = x_d + (x_p - x_d) * lax.rem(lax.rem(x_d, 2) + maj, 2)
        else:
            y_o = yh if m < 2 else 1 - yh
            x_o = 2 * maj + mn * ((3 - 4 * maj) * (1 - h) + h)
        start = ((y_o * 4 + x_o) * 2 + c_d) * 512 + h * 256 + k * LANES
        return pl.ds(pl.multiple_of(start, LANES), LANES)

    def p1(k, h):
        return at(x_=away(h)) if k == 0 else at(x_=near(h))

    def p2(k, h):
        return at(yh_=1 - yh) if k == 0 else at(x_=away(h))

    def halves(body):
        def step(h, carry):
            body(h)
            return carry
        lax.fori_loop(0, 2, step, 0)

    def done(sem, like):
        return pltpu.make_async_copy(like, like, sem)

    own_b = pltpu.make_async_copy(b, bb.at[pl.ds(2 * ROWS, ROWS)], lsem.at[0])
    own_b.start()
    loads = [
        pltpu.make_async_copy(src.at[0, pl.ds(i * 96, 96)], dst.at[pl.ds(i * 96, 96)], ldsem.at[2 * w + i])
        for i in range(2) for w, (src, dst) in enumerate(((g, gb), (e, eb)))
    ]
    for cp in loads:
        cp.start()

    barrier = pltpu.get_barrier_semaphore()
    partners = [at(c_=1 - c), at(x_=na), at(x_=na, c_=1 - c), at(x_=nb), at(x_=nb, c_=1 - c), at(yh_=1 - yh),
                at(yh_=1 - yh, c_=1 - c), at(yl_=1 - yl)] + [at(z_=lax.rem(z + d, 8)) for d in range(1, 8)]
    for p in partners:
        pl.semaphore_signal(barrier, inc=1, device_id=p, device_id_type=MESH)
    off_diagonal = shard != replica

    @pl.when(off_diagonal)
    def _():
        pl.semaphore_signal(barrier, inc=1, device_id=(shard, replica), device_id_type=MESH)

    def maj_of(k, h, m, s):
        return lax.rem(my_maj(k, h, m) + 1 + s, 2)

    def send1(k, h, m, maj):
        return remote(sb.at[k, h, m - 1, maj], cb.at[k, h, maj, rows_of(k, h, m)], s1.at[0], r1.at[k, h, maj],
                      member(k, h, m))

    def correct(k, s):
        for m in (2, 3, 1, 0):
            def one(h):
                maj = maj_of(k, h, m, s)
                for mn in range(2):
                    cols = column(k, h, m, maj, mn)
                    lanes = pl.ds(mn * LANES, LANES)
                    val = (gb[:, cols].astype(F32) + eb[:, cols].astype(F32)).astype(BF16)
                    if m == 0:
                        cb[k, h, maj, rows_of(k, h, 0), lanes] = val
                    else:
                        sb[k, h, m - 1, maj, :, lanes] = val
                if m:
                    send1(k, h, m, maj).start()
            halves(one)

    pl.semaphore_wait(barrier, len(partners) + jnp.where(off_diagonal, 1, 0))

    def slot(i):
        return bb.at[pl.ds(i * ROWS, ROWS)]

    def basis_copy(i, src, dst, dev):
        return remote(slot(src), slot(dst), bsem_s.at[i], bsem_r.at[i], dev)

    core = at(c_=1 - c)
    own_b.wait()
    basis_out = [basis_copy(0, 2, 0, at(x_=na)), basis_copy(1, 2, 4, at(x_=nb)), basis_copy(2, 2, 6, at(yh_=1 - yh)),
                 basis_copy(3, 2, 3, core)]
    basis_on = [basis_copy(4, 0, 1, core), basis_copy(5, 4, 5, core), basis_copy(6, 6, 7, core)]

    def basis_start():
        for cp in basis_out:
            cp.start()

    def turn(first, last):
        def one(i, carry):
            at_ = pl.ds(pl.multiple_of(i * 2 * ROWS, 128), 2 * ROWS)
            bt[:, at_] = bb[at_, :].T
            return carry
        lax.fori_loop(first, last, one, 0)

    def basis_pass(step):
        if step == 0:
            for i in range(3):
                basis_out[i].wait_recv()
                basis_on[i].start()
        elif step == 1:
            basis_out[3].wait_recv()
            for i in range(2):
                basis_on[i].wait_recv()
            turn(0, 3)
        else:
            basis_on[2].wait_recv()
            bb[pl.ds(8 * ROWS, 2 * ROWS), :] = bb[pl.ds(2 * ROWS, 2 * ROWS), :]
            turn(3, 5)

    own_rows = remote(slot(2), bown, bsem_s.at[7], bsem_r.at[7], (shard, replica))
    own_rows_here = pltpu.make_async_copy(slot(2), bown, lsem.at[1])

    def own_start():
        @pl.when(off_diagonal)
        def _():
            own_rows.start()

        @pl.when(shard == replica)
        def _():
            own_rows_here.start()

    def own_wait():
        @pl.when(off_diagonal)
        def _():
            own_rows.wait_recv()

        @pl.when(shard == replica)
        def _():
            own_rows_here.wait()

    def send2(k, h):
        return remote(ps.at[k, h], pr.at[k, h], s2.at[0], r2.at[k, h], p1(k, h))

    def partial(k, s):
        def one(h):
            maj = maj_of(k, h, 0, s)
            done(r1.at[k, h, maj], cb.at[k, h, maj, pl.ds(0, 3 * ROWS)]).wait()

            def tile(i, carry):
                rk = pl.ds(pl.multiple_of(i * 256, 256), 256)
                val = jnp.dot(bt[rk, pl.ds(pl.multiple_of(basis_row(k, h), 128), 4 * ROWS)], cb[k, h, maj],
                              preferred_element_type=F32)
                if s == 0:
                    ps[k, h, rk, :] = val.astype(BF16)
                else:
                    kp[k, h, rk, :] = val
                return carry
            lax.fori_loop(0, 2, tile, 0)
            if s == 0:
                send2(k, h).start()
        halves(one)

    def send3(k, h):
        return remote(xs.at[k, h], xr.at[k, h], s3.at[0], r3.at[k, h], p2(k, h))

    def exchange(k):
        def one(h):
            send2(k, h).wait_recv()
            xs[k, h] = (kp[k, h] + pr[k, h].astype(F32)).astype(BF16)
            send3(k, h).start()
        halves(one)

    def send5(k, h, maj):
        return remote(cf.at[k, h, maj], cf.at[k, h, maj], s5.at[0], r5.at[k, h], p1(k, h))

    def zsend(k, h, d):
        to = lax.rem(z + d, 8)
        return remote(rep.at[k, h, to], rz.at[k, h, d], zs.at[0], zr.at[k, h], at(z_=to))

    def coefficients(k, h):
        maj = my_maj(k, h)
        send3(k, h).wait_recv()
        cf[k, h, maj] = (xs[k, h].astype(F32) + xr[k, h].astype(F32)).astype(BF16)
        mine = cf[k, h, maj, :, pl.ds(pl.multiple_of(my_min(k) * LANES, LANES), LANES)]
        rep[k, h] = mine.reshape(8, 64, LANES)
        send5(k, h, maj).start()
        for d in range(1, 8):
            zsend(k, h, d).start()

    def send6(k, h, m, maj, mn):
        src = er.at[k, h, maj, rows_of(k, h, m), pl.ds(mn * LANES, LANES)]
        return remote(src, o.at[0, :, column(k, h, 0, maj, mn)], s6.at[0], r6.at[0], member(k, h, m))

    def keep6(k, h, maj, mn):
        src = er.at[k, h, maj, rows_of(k, h, 0), pl.ds(mn * LANES, LANES)]
        return pltpu.make_async_copy(src, o.at[0, :, column(k, h, 0, maj, mn)], osem.at[0])

    def rebuild(k, s):
        def one(h):
            maj = lax.rem(my_maj(k, h) + s, 2)
            if s == 1:
                send5(k, h, maj).wait_recv()
            for pair in range(2):
                both = pl.ds(pl.multiple_of(first_of(k, h, pair), 128), 2 * ROWS)
                basis_rows = pl.ds(pl.multiple_of(basis_row(k, h) + first_of(k, h, pair), 128), 2 * ROWS)
                val = jnp.dot(bb[basis_rows, :], cf[k, h, maj], preferred_element_type=F32)
                er[k, h, maj, both, :] = (cb[k, h, maj, both, :].astype(F32) - val).astype(BF16)
                for mn in range(2):
                    if pair == 0:
                        send6(k, h, 2, maj, mn).start()
                        send6(k, h, 3, maj, mn).start()
                    else:
                        send6(k, h, 1, maj, mn).start()
                        keep6(k, h, maj, mn).start()
        halves(one)

    def ysend(k, h):
        return remote(ys.at[k, h], yr.at[k, h], ysm.at[k, h], yrm.at[k, h], at(yl_=1 - yl))

    def z_total(k, h):
        total = rep[k, h, z].astype(F32)
        done(zr.at[k, h], rz.at[k, h, pl.ds(1, 7)]).wait()
        for d in range(1, 8):
            total = total + rz[k, h, d].astype(F32)
        ys[k, h] = total
        ysend(k, h).start()

    def asend(k, h, d):
        return remote(mean.at[k, h, z], mean.at[k, h, z], as_.at[0], ar.at[k, h], at(z_=lax.rem(z + d, 8)))

    def z_mean(k, h):
        ysend(k, h).wait_recv()
        mean[k, h, z] = ((ys[k, h] + yr[k, h]) * (1.0 / 16.0)).astype(BF16)
        for d in range(1, 8):
            asend(k, h, d).start()

    def outer(k, h):
        done(ar.at[k, h], rz.at[k, h, pl.ds(1, 7)]).wait()
        og[:, pl.ds(h * 256 + k * LANES, LANES)] = jnp.dot(
            bown[...], mean[k, h].reshape(RANK, LANES), preferred_element_type=F32)

    for cp in loads:
        cp.wait()
    events = dict(basis_start=basis_start, basis_pass=basis_pass, own_start=own_start, own_wait=own_wait, correct=correct,
                  partial=partial, exchange=exchange, coefficients=coefficients, rebuild=rebuild, z_total=z_total,
                  z_mean=z_mean, outer=outer)
    for name, *where in SCHEDULE:
        events[name](*where)

    for cp in basis_out + basis_on:
        cp.wait_send()

    @pl.when(off_diagonal)
    def _():
        own_rows.wait_send()

    done(s1.at[0], sb).wait()
    done(s2.at[0], ps).wait()
    done(s3.at[0], xs).wait()
    done(s5.at[0], pr).wait()
    for k in range(STAGES):
        for h in range(2):
            ysend(k, h).wait_send()
    done(zs.at[0], rz.at[:, :, pl.ds(1, 7)]).wait()
    done(as_.at[0], rz.at[:, :, pl.ds(1, 7)]).wait()
    done(osem.at[0], er.at[:, :, :, pl.ds(0, ROWS)]).wait()
    done(s6.at[0], sb).wait()
    done(r6.at[0], sb).wait()


def exchange_step(grads, errors, basis):
    K = STAGES
    any_, vmem = pl.BlockSpec(memory_space=pl.ANY), pl.BlockSpec(memory_space=pltpu.VMEM)
    hbm = pl.BlockSpec(memory_space=pltpu.HBM)
    D = pltpu.SemaphoreType.DMA
    V = pltpu.VMEM
    return pl.pallas_call(
        kernel,
        out_shape=(jax.ShapeDtypeStruct(grads.shape, BF16), jax.ShapeDtypeStruct((ROWS, 512), F32)),
        in_specs=[hbm, hbm, hbm],
        out_specs=(any_, vmem),
        scratch_shapes=[
            V((ROWS, 8192), BF16),
            V((ROWS, 8192), BF16),
            V((K, 2, 3, 2, ROWS, 256), BF16),
            V((K, 2, 2, 4 * ROWS, 256), BF16),
            V((10 * ROWS, RANK), BF16),
            V((RANK, 10 * ROWS), BF16),
            V((K, 2, RANK, 256), BF16),
            V((K, 2, RANK, 256), F32),
            V((K, 2, RANK, 256), BF16),
            V((K, 2, RANK, 256), BF16),
            V((K, 2, RANK, 256), BF16),
            V((K, 2, 2, RANK, 256), BF16),
            V((K, 2, 2, 4 * ROWS, 256), BF16),
            V((K, 2, 8, 64, LANES), BF16),
            V((K, 2, 8, 64, LANES), BF16),
            V((K, 2, 64, LANES), F32),
            V((K, 2, 64, LANES), F32),
            V((K, 2, 8, 64, LANES), BF16),
            V((ROWS, RANK), BF16),
            D((4,)),
            D((8,)), D((8,)),
            D((1,)), D((K, 2, 2)),
            D((1,)), D((K, 2)),
            D((1,)), D((K, 2)),
            D((1,)), D((K, 2)),
            D((1,)), D((1,)),
            D((1,)), D((K, 2)),
            D((K, 2)), D((K, 2)),
            D((1,)), D((K, 2)),
            D((1,)),
            D((2,)),
        ],
        compiler_params=pltpu.CompilerParams(
            collective_id=0, has_side_effects=True, vmem_limit_bytes=40 << 20),
        name="exchange_step",
    )(*(pltpu.with_memory_space_constraint(a, pltpu.HBM) for a in (grads, errors, basis)))


def body(grads, errors, basis, params, momentum):
    new_error, outer_grad = exchange_step(grads, errors, basis)
    new_momentum = momentum_rate * momentum + outer_grad
    new_params = params - outer_rate * (outer_grad + momentum_rate * new_momentum)
    return (new_params, new_momentum, new_error)


def solution(mesh):
    in_specs = (
        P("replica", "shard", None),
        P("replica", "shard", None),
        P("shard", None),
        P("replica", "shard"),
        P("replica", "shard"),
    )
    out_specs = (P("replica", "shard"), P("replica", "shard"), P("replica", "shard", None))
    return jax.shard_map(body, mesh=mesh, in_specs=in_specs, out_specs=out_specs, check_vma=False)
```

```python
import jax
import jax.numpy as jnp
from jax import lax
from jax.experimental import pallas as pl
from jax.experimental.pallas import tpu as pltpu
from jax.sharding import PartitionSpec as P

momentum_rate = 0.9
outer_rate = 0.7
MESH = pl.DeviceIdType.MESH
F32, BF16 = jnp.float32, jnp.bfloat16

STAGES = 2
ROWS, RANK, LANES = 192, 512, 128
SCHEDULE = (
    ("basis_start",),
    ("correct", 0, 0),
    ("correct", 1, 0),
    ("correct", 0, 1),
    ("correct", 1, 1),
    ("basis_pass", 0),
    ("basis_pass", 1),
    ("partial", 0, 0),
    ("basis_pass", 2),
    ("partial", 0, 1),
    ("partial", 1, 0),
    ("own_start",),
    ("exchange", 0),
    ("partial", 1, 1),
    ("exchange", 1),
    ("own_relay",),
    ("coefficients", 0, 0),
    ("coefficients", 1, 0),
    ("coefficients", 1, 1),
    ("rebuild", 1, 0, 0),
    ("coefficients", 0, 1),
    ("z_total", 0, 0),
    ("rebuild", 1, 0, 1),
    ("z_total", 1, 0),
    ("rebuild", 0, 0, 0),
    ("z_total", 1, 1),
    ("z_mean", 0, 0),
    ("rebuild", 0, 0, 1),
    ("rebuild", 1, 1, 0),
    ("z_total", 0, 1),
    ("z_mean", 1, 0),
    ("rebuild", 1, 1, 1),
    ("z_mean", 1, 1),
    ("rebuild", 0, 1, 0),
    ("z_mean", 0, 1),
    ("rebuild", 0, 1, 1),
    ("own_wait",),
    ("outer", 0, 0),
    ("outer", 1, 0),
    ("outer", 1, 1),
    ("outer", 0, 1),
)


def kernel(g, e, b, o, og, gb, eb, sb, cb, bb, bt, ps, kp, pr, xs, xr, cf, er, rep, rz, ys, yr, mean,
           ldsem, bsem_s, bsem_r, s1, r1, s2, r2, s3, r3, s5, r5, s6, r6, zs, zr, ysm, yrm, as_, ar, osem, lsem):
    shard, replica = lax.axis_index("shard"), lax.axis_index("replica")
    yh, x, c = shard // 8, lax.rem(shard // 2, 4), lax.rem(shard, 2)
    yl, z = replica // 8, lax.rem(replica, 8)
    par = lax.rem(x, 2)
    na = x + 1 - 2 * par
    nb = lax.rem(x + 3 + 2 * par, 4)

    def at(yh_=None, x_=None, c_=None, yl_=None, z_=None):
        yh_ = yh if yh_ is None else yh_
        x_ = x if x_ is None else x_
        c_ = c if c_ is None else c_
        yl_ = yl if yl_ is None else yl_
        z_ = z if z_ is None else z_
        return (yl_ * 8 + z_, (yh_ * 4 + x_) * 2 + c_)

    def remote(src, dst, ss, rs, dev):
        return pltpu.make_async_remote_copy(
            src_ref=src, dst_ref=dst, send_sem=ss, recv_sem=rs, device_id=dev, device_id_type=MESH)

    def near(h):
        return na + h * (nb - na)

    def away(h):
        return nb + h * (na - nb)

    def member(k, h, m):
        c_m = c if m % 2 == 0 else 1 - c
        if m < 2:
            return at(c_=c_m)
        return at(x_=near(h), c_=c_m) if k == 0 else at(yh_=1 - yh, c_=c_m)

    def first_of(k, h, pair):
        if k == 1:
            return pair * 2 * ROWS
        return (h if pair == 0 else 1 - h) * 2 * ROWS

    def basis_row(k, h):
        return h * 2 * ROWS if k == 0 else 6 * ROWS

    def rows_of(k, h, m):
        row = first_of(k, h, 0 if m >= 2 else 1) + (m % 2) * ROWS
        return pl.ds(pl.multiple_of(row, ROWS), ROWS)

    def my_maj(k, h, m=0):
        if k == 0:
            return par if m < 2 else 1 - par
        odd = lax.rem((x + 1) // 2, 2)
        return odd + h * (x // 2 - odd)

    def my_min(k):
        return yh if k == 0 else par

    def column(k, h, m, maj, mn):
        c_d = c if m % 2 == 0 else 1 - c
        if k == 0:
            x_d = x if m < 2 else near(h)
            x_p = away(h) if m < 2 else lax.rem(x + 2, 4)
            y_o = mn
            x_o = x_d + (x_p - x_d) * lax.rem(lax.rem(x_d, 2) + maj, 2)
        else:
            y_o = yh if m < 2 else 1 - yh
            x_o = 2 * maj + mn * ((3 - 4 * maj) * (1 - h) + h)
        start = ((y_o * 4 + x_o) * 2 + c_d) * 512 + h * 256 + k * LANES
        return pl.ds(pl.multiple_of(start, LANES), LANES)

    def p1(k, h):
        return at(x_=away(h)) if k == 0 else at(x_=near(h))

    def p2(k, h):
        return at(yh_=1 - yh) if k == 0 else at(x_=away(h))

    def halves(body):
        def step(h, carry):
            body(h)
            return carry
        lax.fori_loop(0, 2, step, 0)

    def done(sem, like):
        return pltpu.make_async_copy(like, like, sem)

    own_b = pltpu.make_async_copy(b, bb.at[pl.ds(2 * ROWS, ROWS)], lsem.at[0])
    own_b.start()
    loads = [
        pltpu.make_async_copy(src.at[0, pl.ds(i * 96, 96)], dst.at[pl.ds(i * 96, 96)], ldsem.at[2 * w + i])
        for i in range(2) for w, (src, dst) in enumerate(((g, gb), (e, eb)))
    ]
    for cp in loads:
        cp.start()

    barrier = pltpu.get_barrier_semaphore()
    partners = [at(c_=1 - c), at(x_=na), at(x_=na, c_=1 - c), at(x_=nb), at(x_=nb, c_=1 - c), at(yh_=1 - yh),
                at(yh_=1 - yh, c_=1 - c), at(yl_=1 - yl)] + [at(z_=lax.rem(z + d, 8)) for d in range(1, 8)]
    for p in partners:
        pl.semaphore_signal(barrier, inc=1, device_id=p, device_id_type=MESH)
    def maj_of(k, h, m, s):
        return lax.rem(my_maj(k, h, m) + 1 + s, 2)

    def send1(k, h, m, maj):
        return remote(sb.at[k, h, m - 1, maj], cb.at[k, h, maj, rows_of(k, h, m)], s1.at[0], r1.at[k, h, maj],
                      member(k, h, m))

    def correct(k, s):
        for m in (2, 3, 1, 0):
            def one(h):
                maj = maj_of(k, h, m, s)
                for mn in range(2):
                    cols = column(k, h, m, maj, mn)
                    lanes = pl.ds(mn * LANES, LANES)
                    val = (gb[:, cols].astype(F32) + eb[:, cols].astype(F32)).astype(BF16)
                    if m == 0:
                        cb[k, h, maj, rows_of(k, h, 0), lanes] = val
                    else:
                        sb[k, h, m - 1, maj, :, lanes] = val
                if m:
                    send1(k, h, m, maj).start()
            halves(one)

    pl.semaphore_wait(barrier, len(partners))

    def slot(i):
        return bb.at[pl.ds(i * ROWS, ROWS)]

    def basis_copy(i, src, dst, dev):
        return remote(slot(src), slot(dst), bsem_s.at[i], bsem_r.at[i], dev)

    core = at(c_=1 - c)
    own_b.wait()
    basis_out = [basis_copy(0, 2, 0, at(x_=na)), basis_copy(1, 2, 4, at(x_=nb)), basis_copy(2, 2, 6, at(yh_=1 - yh)),
                 basis_copy(3, 2, 3, core)]
    basis_on = [basis_copy(4, 0, 1, core), basis_copy(5, 4, 5, core), basis_copy(6, 6, 7, core)]

    def basis_start():
        for cp in basis_out:
            cp.start()

    def turn(first, last):
        def one(i, carry):
            at_ = pl.ds(pl.multiple_of(i * 2 * ROWS, 128), 2 * ROWS)
            bt[:, at_] = bb[at_, :].T
            return carry
        lax.fori_loop(first, last, one, 0)

    def basis_pass(step):
        if step == 0:
            for i in range(3):
                basis_out[i].wait_recv()
                basis_on[i].start()
        elif step == 1:
            basis_out[3].wait_recv()
            for i in range(2):
                basis_on[i].wait_recv()
            turn(0, 3)
        else:
            basis_on[2].wait_recv()
            bb[pl.ds(8 * ROWS, 2 * ROWS), :] = bb[pl.ds(2 * ROWS, 2 * ROWS), :]
            turn(3, 5)

    side = lax.rem(z // 2 - x + 4, 4)
    other = lax.rem(lax.rem(z, 2) + c, 2)
    level = lax.rem(yh + yl, 2)
    near_slot = jnp.where(side == 0, 2, jnp.where(side == 1, 4 * par, 4 - 4 * par)) + other
    far = jnp.logical_or(jnp.logical_and(level == 0, side == 2), jnp.logical_and(level == 1, side != 0))
    own_slot = jnp.where(far, 10, jnp.where(level == 0, near_slot, 6 + other))
    to_right = jnp.logical_or(jnp.logical_and(level == 0, side == 3), jnp.logical_and(level == 1, side == 0))
    to_left = jnp.logical_and(level == 1, side == 0)
    on_right = jnp.logical_and(level == 1, side == 3)
    right, left = at(x_=lax.rem(x + 1, 4)), at(x_=lax.rem(x + 3, 4))

    def part(row, half):
        return bb.at[pl.ds(pl.multiple_of(row * ROWS + half * 96, 96), 96)]

    own_right = remote(part(own_slot, c), part(10, c), bsem_s.at[7], bsem_r.at[7], right)
    own_left = remote(part(own_slot, c), part(10, c), bsem_s.at[8], bsem_r.at[7], left)
    own_core = remote(part(10, c), part(10, c), bsem_s.at[9], bsem_r.at[8], core)

    def own_start():
        @pl.when(to_right)
        def _():
            own_right.start()

        @pl.when(to_left)
        def _():
            own_left.start()

    def own_relay():
        @pl.when(far)
        def _():
            own_right.wait_recv()
            own_core.start()

        @pl.when(on_right)
        def _():
            own_right.start()

    def own_wait():
        @pl.when(far)
        def _():
            own_core.wait_recv()

    def own_end():
        @pl.when(jnp.logical_or(to_right, on_right))
        def _():
            own_right.wait_send()

        @pl.when(to_left)
        def _():
            own_left.wait_send()

        @pl.when(far)
        def _():
            own_core.wait_send()

    def send2(k, h):
        return remote(ps.at[k, h], pr.at[k, h], s2.at[0], r2.at[k, h], p1(k, h))

    def partial(k, s):
        def one(h):
            maj = maj_of(k, h, 0, s)
            done(r1.at[k, h, maj], cb.at[k, h, maj, pl.ds(0, 3 * ROWS)]).wait()

            def tile(i, carry):
                rk = pl.ds(pl.multiple_of(i * 256, 256), 256)
                val = jnp.dot(bt[rk, pl.ds(pl.multiple_of(basis_row(k, h), 128), 4 * ROWS)], cb[k, h, maj],
                              preferred_element_type=F32)
                if s == 0:
                    ps[k, h, rk, :] = val.astype(BF16)
                else:
                    kp[k, h, rk, :] = val
                return carry
            lax.fori_loop(0, 2, tile, 0)
            if s == 0:
                send2(k, h).start()
        halves(one)

    def send3(k, h):
        return remote(xs.at[k, h], xr.at[k, h], s3.at[0], r3.at[k, h], p2(k, h))

    def exchange(k):
        def one(h):
            send2(k, h).wait_recv()
            xs[k, h] = (kp[k, h] + pr[k, h].astype(F32)).astype(BF16)
            send3(k, h).start()
        halves(one)

    def send5(k, h, maj):
        return remote(cf.at[k, h, maj], cf.at[k, h, maj], s5.at[0], r5.at[k, h], p1(k, h))

    def zsend(k, h, d):
        to = lax.rem(z + d, 8)
        return remote(rep.at[k, h, to], rz.at[k, h, d], zs.at[0], zr.at[k, h], at(z_=to))

    def coefficients(k, h):
        maj = my_maj(k, h)
        send3(k, h).wait_recv()
        cf[k, h, maj] = (xs[k, h].astype(F32) + xr[k, h].astype(F32)).astype(BF16)
        mine = cf[k, h, maj, :, pl.ds(pl.multiple_of(my_min(k) * LANES, LANES), LANES)]
        rep[k, h] = mine.reshape(8, 64, LANES)
        send5(k, h, maj).start()
        for d in range(1, 8):
            zsend(k, h, d).start()

    def send6(k, h, m, maj, mn):
        src = er.at[k, h, maj, rows_of(k, h, m), pl.ds(mn * LANES, LANES)]
        return remote(src, o.at[0, :, column(k, h, 0, maj, mn)], s6.at[0], r6.at[0], member(k, h, m))

    def keep6(k, h, maj, mn):
        src = er.at[k, h, maj, rows_of(k, h, 0), pl.ds(mn * LANES, LANES)]
        return pltpu.make_async_copy(src, o.at[0, :, column(k, h, 0, maj, mn)], osem.at[0])

    def rebuild(k, s, h):
        maj = lax.rem(my_maj(k, h) + s, 2)
        if s == 1:
            send5(k, h, maj).wait_recv()
        for pair in range(2):
            both = pl.ds(pl.multiple_of(first_of(k, h, pair), 128), 2 * ROWS)
            basis_rows = pl.ds(pl.multiple_of(basis_row(k, h) + first_of(k, h, pair), 128), 2 * ROWS)
            val = jnp.dot(bb[basis_rows, :], cf[k, h, maj], preferred_element_type=F32)
            er[k, h, maj, both, :] = (cb[k, h, maj, both, :].astype(F32) - val).astype(BF16)
            for mn in range(2):
                if pair == 0:
                    send6(k, h, 2, maj, mn).start()
                    send6(k, h, 3, maj, mn).start()
                else:
                    send6(k, h, 1, maj, mn).start()
                    keep6(k, h, maj, mn).start()

    def ysend(k, h):
        return remote(ys.at[k, h], yr.at[k, h], ysm.at[k, h], yrm.at[k, h], at(yl_=1 - yl))

    def z_total(k, h):
        total = rep[k, h, z].astype(F32)
        done(zr.at[k, h], rz.at[k, h, pl.ds(1, 7)]).wait()
        for d in range(1, 8):
            total = total + rz[k, h, d].astype(F32)
        ys[k, h] = total
        ysend(k, h).start()

    def asend(k, h, d):
        return remote(mean.at[k, h, z], mean.at[k, h, z], as_.at[0], ar.at[k, h], at(z_=lax.rem(z + d, 8)))

    def z_mean(k, h):
        ysend(k, h).wait_recv()
        mean[k, h, z] = ((ys[k, h] + yr[k, h]) * (1.0 / 16.0)).astype(BF16)
        for d in range(1, 8):
            asend(k, h, d).start()

    def outer(k, h):
        done(ar.at[k, h], rz.at[k, h, pl.ds(1, 7)]).wait()
        og[:, pl.ds(h * 256 + k * LANES, LANES)] = jnp.dot(
            bb[pl.ds(pl.multiple_of(own_slot * ROWS, ROWS), ROWS), :], mean[k, h].reshape(RANK, LANES), preferred_element_type=F32)

    for cp in loads:
        cp.wait()
    events = dict(basis_start=basis_start, basis_pass=basis_pass, own_start=own_start, own_relay=own_relay, own_wait=own_wait, correct=correct,
                  partial=partial, exchange=exchange, coefficients=coefficients, rebuild=rebuild, z_total=z_total,
                  z_mean=z_mean, outer=outer)
    for name, *where in SCHEDULE:
        events[name](*where)

    for cp in basis_out + basis_on:
        cp.wait_send()

    own_end()

    done(s1.at[0], sb).wait()
    done(s2.at[0], ps).wait()
    done(s3.at[0], xs).wait()
    done(s5.at[0], pr).wait()
    for k in range(STAGES):
        for h in range(2):
            ysend(k, h).wait_send()
    done(zs.at[0], rz.at[:, :, pl.ds(1, 7)]).wait()
    done(as_.at[0], rz.at[:, :, pl.ds(1, 7)]).wait()
    done(osem.at[0], er.at[:, :, :, pl.ds(0, ROWS)]).wait()
    done(s6.at[0], sb).wait()
    done(r6.at[0], sb).wait()


def exchange_step(grads, errors, basis):
    K = STAGES
    any_, vmem = pl.BlockSpec(memory_space=pl.ANY), pl.BlockSpec(memory_space=pltpu.VMEM)
    hbm = pl.BlockSpec(memory_space=pltpu.HBM)
    D = pltpu.SemaphoreType.DMA
    V = pltpu.VMEM
    return pl.pallas_call(
        kernel,
        out_shape=(jax.ShapeDtypeStruct(grads.shape, BF16), jax.ShapeDtypeStruct((ROWS, 512), F32)),
        in_specs=[hbm, hbm, hbm],
        out_specs=(any_, vmem),
        scratch_shapes=[
            V((ROWS, 8192), BF16),
            V((ROWS, 8192), BF16),
            V((K, 2, 3, 2, ROWS, 256), BF16),
            V((K, 2, 2, 4 * ROWS, 256), BF16),
            V((11 * ROWS, RANK), BF16),
            V((RANK, 10 * ROWS), BF16),
            V((K, 2, RANK, 256), BF16),
            V((K, 2, RANK, 256), F32),
            V((K, 2, RANK, 256), BF16),
            V((K, 2, RANK, 256), BF16),
            V((K, 2, RANK, 256), BF16),
            V((K, 2, 2, RANK, 256), BF16),
            V((K, 2, 2, 4 * ROWS, 256), BF16),
            V((K, 2, 8, 64, LANES), BF16),
            V((K, 2, 8, 64, LANES), BF16),
            V((K, 2, 64, LANES), F32),
            V((K, 2, 64, LANES), F32),
            V((K, 2, 8, 64, LANES), BF16),
            D((4,)),
            D((10,)), D((9,)),
            D((1,)), D((K, 2, 2)),
            D((1,)), D((K, 2)),
            D((1,)), D((K, 2)),
            D((1,)), D((K, 2)),
            D((1,)), D((1,)),
            D((1,)), D((K, 2)),
            D((K, 2)), D((K, 2)),
            D((1,)), D((K, 2)),
            D((1,)),
            D((1,)),
        ],
        compiler_params=pltpu.CompilerParams(
            collective_id=0, has_side_effects=True, vmem_limit_bytes=40 << 20),
        name="exchange_step",
    )(*(pltpu.with_memory_space_constraint(a, pltpu.HBM) for a in (grads, errors, basis)))


def body(grads, errors, basis, params, momentum):
    new_error, outer_grad = exchange_step(grads, errors, basis)
    new_momentum = momentum_rate * momentum + outer_grad
    new_params = params - outer_rate * (outer_grad + momentum_rate * new_momentum)
    return (new_params, new_momentum, new_error)


def solution(mesh):
    in_specs = (
        P("replica", "shard", None),
        P("replica", "shard", None),
        P("shard", None),
        P("replica", "shard"),
        P("replica", "shard"),
    )
    out_specs = (P("replica", "shard"), P("replica", "shard"), P("replica", "shard", None))
    return jax.shard_map(body, mesh=mesh, in_specs=in_specs, out_specs=out_specs, check_vma=False)
```

```python
import jax
import jax.numpy as jnp
from jax import lax
from jax.experimental import pallas as pl
from jax.experimental.pallas import tpu as pltpu
from jax.sharding import PartitionSpec as P

momentum_rate = 0.9
outer_rate = 0.7
MESH = pl.DeviceIdType.MESH
F32, BF16 = jnp.float32, jnp.bfloat16

STAGES = 2
ROWS, RANK, LANES = 192, 512, 128
SCHEDULE = (
    ("basis_start",),
    ("correct", 0, 0),
    ("correct", 1, 0),
    ("basis_pass", 0),
    ("correct", 0, 1),
    ("correct", 1, 1),
    ("basis_pass", 1),
    ("partial", 0, 0),
    ("basis_pass", 2),
    ("partial", 0, 1),
    ("partial", 1, 0),
    ("own_start",),
    ("exchange", 0),
    ("partial", 1, 1),
    ("exchange", 1),
    ("own_relay",),
    ("coefficients", 0, 0),
    ("rebuild", 0, 0, 0),
    ("coefficients", 1, 0),
    ("coefficients", 1, 1),
    ("coefficients", 0, 1),
    ("rebuild", 1, 0, 0),
    ("z_total", 0, 0),
    ("rebuild", 1, 0, 1),
    ("rebuild", 0, 0, 1),
    ("z_total", 1, 0),
    ("z_total", 1, 1),
    ("z_mean", 0, 0),
    ("z_total", 0, 1),
    ("rebuild", 1, 1, 0),
    ("z_mean", 1, 0),
    ("z_mean", 1, 1),
    ("rebuild", 1, 1, 1),
    ("z_mean", 0, 1),
    ("rebuild", 0, 1, 0),
    ("rebuild", 0, 1, 1),
    ("own_wait",),
    ("outer", 0, 0),
    ("outer", 1, 0),
    ("outer", 1, 1),
    ("outer", 0, 1),
)


def kernel(g, e, b, o, og, gb, eb, sb, cb, bb, bt, ps, kp, pr, xs, xr, cf, er, rep, rz, ys, yr, mean,
           ldsem, bsem_s, bsem_r, s1, r1, s2, r2, s3, r3, s5, r5, s6, r6, zs, zr, ysm, yrm, as_, ar, osem, lsem):
    shard, replica = lax.axis_index("shard"), lax.axis_index("replica")
    yh, x, c = shard // 8, lax.rem(shard // 2, 4), lax.rem(shard, 2)
    yl, z = replica // 8, lax.rem(replica, 8)
    par = lax.rem(x, 2)
    na = x + 1 - 2 * par
    nb = lax.rem(x + 3 + 2 * par, 4)

    def at(yh_=None, x_=None, c_=None, yl_=None, z_=None):
        yh_ = yh if yh_ is None else yh_
        x_ = x if x_ is None else x_
        c_ = c if c_ is None else c_
        yl_ = yl if yl_ is None else yl_
        z_ = z if z_ is None else z_
        return (yl_ * 8 + z_, (yh_ * 4 + x_) * 2 + c_)

    def remote(src, dst, ss, rs, dev):
        return pltpu.make_async_remote_copy(
            src_ref=src, dst_ref=dst, send_sem=ss, recv_sem=rs, device_id=dev, device_id_type=MESH)

    def near(h):
        return na + h * (nb - na)

    def away(h):
        return nb + h * (na - nb)

    def member(k, h, m):
        c_m = c if m % 2 == 0 else 1 - c
        if m < 2:
            return at(c_=c_m)
        return at(x_=near(h), c_=c_m) if k == 0 else at(yh_=1 - yh, c_=c_m)

    def first_of(k, h, pair):
        if k == 1:
            return pair * 2 * ROWS
        return (h if pair == 0 else 1 - h) * 2 * ROWS

    def basis_row(k, h):
        return h * 2 * ROWS if k == 0 else 6 * ROWS

    def rows_of(k, h, m):
        row = first_of(k, h, 0 if m >= 2 else 1) + (m % 2) * ROWS
        return pl.ds(pl.multiple_of(row, ROWS), ROWS)

    def my_maj(k, h, m=0):
        if k == 0:
            return par if m < 2 else 1 - par
        odd = lax.rem((x + 1) // 2, 2)
        return odd + h * (x // 2 - odd)

    def my_min(k):
        return yh if k == 0 else par

    def column(k, h, m, maj, mn):
        c_d = c if m % 2 == 0 else 1 - c
        if k == 0:
            x_d = x if m < 2 else near(h)
            x_p = away(h) if m < 2 else lax.rem(x + 2, 4)
            y_o = mn
            x_o = x_d + (x_p - x_d) * lax.rem(lax.rem(x_d, 2) + maj, 2)
        else:
            y_o = yh if m < 2 else 1 - yh
            x_o = 2 * maj + mn * ((3 - 4 * maj) * (1 - h) + h)
        start = ((y_o * 4 + x_o) * 2 + c_d) * 512 + h * 256 + k * LANES
        return pl.ds(pl.multiple_of(start, LANES), LANES)

    def p1(k, h):
        return at(x_=away(h)) if k == 0 else at(x_=near(h))

    def p2(k, h):
        return at(yh_=1 - yh) if k == 0 else at(x_=away(h))

    def halves(body):
        def step(h, carry):
            body(h)
            return carry
        lax.fori_loop(0, 2, step, 0)

    def done(sem, like):
        return pltpu.make_async_copy(like, like, sem)

    own_b = pltpu.make_async_copy(b, bb.at[pl.ds(2 * ROWS, ROWS)], lsem.at[0])
    own_b.start()
    loads = [
        pltpu.make_async_copy(src.at[0, pl.ds(i * 96, 96)], dst.at[pl.ds(i * 96, 96)], ldsem.at[2 * w + i])
        for i in range(2) for w, (src, dst) in enumerate(((g, gb), (e, eb)))
    ]
    for cp in loads:
        cp.start()

    barrier = pltpu.get_barrier_semaphore()
    partners = [at(c_=1 - c), at(x_=na), at(x_=na, c_=1 - c), at(x_=nb), at(x_=nb, c_=1 - c), at(yh_=1 - yh),
                at(yh_=1 - yh, c_=1 - c), at(yl_=1 - yl)] + [at(z_=lax.rem(z + d, 8)) for d in range(1, 8)]
    for p in partners:
        pl.semaphore_signal(barrier, inc=1, device_id=p, device_id_type=MESH)
    def maj_of(k, h, m, s):
        return lax.rem(my_maj(k, h, m) + 1 + s, 2)

    def send1(k, h, m, maj):
        return remote(sb.at[k, h, m - 1, maj], cb.at[k, h, maj, rows_of(k, h, m)], s1.at[0], r1.at[k, h, maj],
                      member(k, h, m))

    def correct(k, s):
        for m in (2, 3, 1, 0):
            def one(h):
                maj = maj_of(k, h, m, s)
                for mn in range(2):
                    cols = column(k, h, m, maj, mn)
                    lanes = pl.ds(mn * LANES, LANES)
                    val = (gb[:, cols].astype(F32) + eb[:, cols].astype(F32)).astype(BF16)
                    if m == 0:
                        cb[k, h, maj, rows_of(k, h, 0), lanes] = val
                    else:
                        sb[k, h, m - 1, maj, :, lanes] = val
                if m:
                    send1(k, h, m, maj).start()
            halves(one)

    pl.semaphore_wait(barrier, len(partners))

    def slot(i):
        return bb.at[pl.ds(i * ROWS, ROWS)]

    odd_z = lax.rem(z, 2)
    z_one, z_two = at(z_=z + 1 - 2 * odd_z), at(z_=lax.rem(z + 7 + 2 * odd_z, 8))

    def half(i, which):
        return bb.at[pl.ds(pl.multiple_of(i * ROWS + which * 96, 96), 96)]

    def basis_copy(i, src, dst, dev):
        return remote(src, dst, bsem_s.at[i], bsem_r.at[i], dev)

    core = at(c_=1 - c)
    own_b.wait()
    basis_out, basis_z, basis_z_in, basis_on, basis_on_z = [], [], [], [], []
    for i, (n, dev, zdev) in enumerate(((0, at(x_=na), z_one), (4, at(x_=nb), z_two), (6, at(yh_=1 - yh), z_one))):
        basis_out.append(basis_copy(4 * i, half(2, odd_z), half(n, odd_z), dev))
        basis_z.append(basis_copy(4 * i + 1, half(n, odd_z), half(n, odd_z), zdev))
        basis_z_in.append(basis_copy(4 * i + 1, half(n, 1 - odd_z), half(n, 1 - odd_z), zdev))
        basis_on.append(basis_copy(4 * i + 2, half(n, odd_z), half(n + 1, odd_z), core))
        basis_on_z.append(basis_copy(4 * i + 3, half(n, 1 - odd_z), half(n + 1, 1 - odd_z), core))
    basis_core = basis_copy(12, slot(2), slot(3), core)

    def basis_start():
        for cp in basis_out:
            cp.start()
        basis_core.start()
        for cp in loads:
            cp.wait()

    def turn(first, last):
        def one(i, carry):
            at_ = pl.ds(pl.multiple_of(i * 2 * ROWS, 128), 2 * ROWS)
            bt[:, at_] = bb[at_, :].T
            return carry
        lax.fori_loop(first, last, one, 0)

    def basis_pass(step):
        if step == 0:
            for i in range(3):
                basis_out[i].wait_recv()
                basis_z[i].start()
                basis_on[i].start()
        else:
            for i in range(2) if step == 1 else (2,):
                basis_z_in[i].wait_recv()
                basis_on_z[i].start()
            if step == 1:
                basis_core.wait_recv()
            for i in range(2) if step == 1 else (2,):
                basis_on[i].wait_recv()
                basis_on_z[i].wait_recv()
            if step == 1:
                turn(0, 3)
            else:
                bb[pl.ds(8 * ROWS, 2 * ROWS), :] = bb[pl.ds(2 * ROWS, 2 * ROWS), :]
                turn(3, 5)

    side = lax.rem(z // 2 - x + 4, 4)
    other = lax.rem(lax.rem(z, 2) + c, 2)
    level = lax.rem(yh + yl, 2)
    near_slot = jnp.where(side == 0, 2, jnp.where(side == 1, 4 * par, 4 - 4 * par)) + other
    far = jnp.logical_or(jnp.logical_and(level == 0, side == 2), jnp.logical_and(level == 1, side != 0))
    own_slot = jnp.where(far, 10, jnp.where(level == 0, near_slot, 6 + other))
    to_right = jnp.logical_or(jnp.logical_and(level == 0, side == 3), jnp.logical_and(level == 1, side == 0))
    to_left = jnp.logical_and(level == 1, side == 0)
    on_right = jnp.logical_and(level == 1, side == 3)
    right, left = at(x_=lax.rem(x + 1, 4)), at(x_=lax.rem(x + 3, 4))

    def part(row, half):
        return bb.at[pl.ds(pl.multiple_of(row * ROWS + half * 96, 96), 96)]

    own_right = remote(part(own_slot, c), part(10, c), bsem_s.at[13], bsem_r.at[13], right)
    own_left = remote(part(own_slot, c), part(10, c), bsem_s.at[14], bsem_r.at[13], left)
    own_core = remote(part(10, c), part(10, c), bsem_s.at[15], bsem_r.at[14], core)

    def own_start():
        @pl.when(to_right)
        def _():
            own_right.start()

        @pl.when(to_left)
        def _():
            own_left.start()

    def own_relay():
        @pl.when(far)
        def _():
            own_right.wait_recv()
            own_core.start()

        @pl.when(on_right)
        def _():
            own_right.start()

    def own_wait():
        @pl.when(far)
        def _():
            own_core.wait_recv()

    def own_end():
        @pl.when(jnp.logical_or(to_right, on_right))
        def _():
            own_right.wait_send()

        @pl.when(to_left)
        def _():
            own_left.wait_send()

        @pl.when(far)
        def _():
            own_core.wait_send()

    def send2(k, h):
        return remote(ps.at[k, h], pr.at[k, h], s2.at[0], r2.at[k, h], p1(k, h))

    def partial(k, s):
        def one(h):
            maj = maj_of(k, h, 0, s)
            done(r1.at[k, h, maj], cb.at[k, h, maj, pl.ds(0, 3 * ROWS)]).wait()

            def tile(i, carry):
                rk = pl.ds(pl.multiple_of(i * 256, 256), 256)
                val = jnp.dot(bt[rk, pl.ds(pl.multiple_of(basis_row(k, h), 128), 4 * ROWS)], cb[k, h, maj],
                              preferred_element_type=F32)
                if s == 0:
                    ps[k, h, rk, :] = val.astype(BF16)
                else:
                    kp[k, h, rk, :] = val
                return carry
            lax.fori_loop(0, 2, tile, 0)
            if s == 0:
                send2(k, h).start()
        halves(one)

    def send3(k, h):
        return remote(xs.at[k, h], xr.at[k, h], s3.at[0], r3.at[k, h], p2(k, h))

    def exchange(k):
        def one(h):
            send2(k, h).wait_recv()
            xs[k, h] = (kp[k, h] + pr[k, h].astype(F32)).astype(BF16)
            send3(k, h).start()
        halves(one)

    def send5(k, h, maj):
        return remote(cf.at[k, h, maj], cf.at[k, h, maj], s5.at[0], r5.at[k, h], p1(k, h))

    def zsend(k, h, d):
        to = lax.rem(z + d, 8)
        return remote(rep.at[k, h, to], rz.at[k, h, d], zs.at[0], zr.at[k, h], at(z_=to))

    def coefficients(k, h):
        maj = my_maj(k, h)
        send3(k, h).wait_recv()
        cf[k, h, maj] = (xs[k, h].astype(F32) + xr[k, h].astype(F32)).astype(BF16)
        mine = cf[k, h, maj, :, pl.ds(pl.multiple_of(my_min(k) * LANES, LANES), LANES)]
        rep[k, h] = mine.reshape(8, 64, LANES)
        for d in range(1, 8):
            zsend(k, h, d).start()
        send5(k, h, maj).start()

    def send6(k, h, m, maj, mn):
        src = er.at[k, h, maj, rows_of(k, h, m), pl.ds(mn * LANES, LANES)]
        return remote(src, o.at[0, :, column(k, h, 0, maj, mn)], s6.at[0], r6.at[0], member(k, h, m))

    def keep6(k, h, maj, mn):
        src = er.at[k, h, maj, rows_of(k, h, 0), pl.ds(mn * LANES, LANES)]
        return pltpu.make_async_copy(src, o.at[0, :, column(k, h, 0, maj, mn)], osem.at[0])

    def rebuild(k, s, h):
        maj = lax.rem(my_maj(k, h) + s, 2)
        if s == 1:
            send5(k, h, maj).wait_recv()
        for pair in range(2):
            both = pl.ds(pl.multiple_of(first_of(k, h, pair), 128), 2 * ROWS)
            basis_rows = pl.ds(pl.multiple_of(basis_row(k, h) + first_of(k, h, pair), 128), 2 * ROWS)
            val = jnp.dot(bb[basis_rows, :], cf[k, h, maj], preferred_element_type=F32)
            er[k, h, maj, both, :] = (cb[k, h, maj, both, :].astype(F32) - val).astype(BF16)
            for mn in range(2):
                if pair == 0:
                    send6(k, h, 2, maj, mn).start()
                    send6(k, h, 3, maj, mn).start()
                else:
                    send6(k, h, 1, maj, mn).start()
                    keep6(k, h, maj, mn).start()

    def ysend(k, h):
        return remote(ys.at[k, h], yr.at[k, h], ysm.at[k, h], yrm.at[k, h], at(yl_=1 - yl))

    def z_total(k, h):
        total = rep[k, h, z].astype(F32)
        done(zr.at[k, h], rz.at[k, h, pl.ds(1, 7)]).wait()
        for d in range(1, 8):
            total = total + rz[k, h, d].astype(F32)
        ys[k, h] = total
        ysend(k, h).start()

    def asend(k, h, d):
        return remote(mean.at[k, h, z], mean.at[k, h, z], as_.at[0], ar.at[k, h], at(z_=lax.rem(z + d, 8)))

    def z_mean(k, h):
        ysend(k, h).wait_recv()
        mean[k, h, z] = ((ys[k, h] + yr[k, h]) * (1.0 / 16.0)).astype(BF16)
        for d in range(1, 8):
            asend(k, h, d).start()

    def outer(k, h):
        done(ar.at[k, h], rz.at[k, h, pl.ds(1, 7)]).wait()
        og[:, pl.ds(h * 256 + k * LANES, LANES)] = jnp.dot(
            bb[pl.ds(pl.multiple_of(own_slot * ROWS, ROWS), ROWS), :], mean[k, h].reshape(RANK, LANES), preferred_element_type=F32)

    events = dict(basis_start=basis_start, basis_pass=basis_pass, own_start=own_start, own_relay=own_relay, own_wait=own_wait, correct=correct,
                  partial=partial, exchange=exchange, coefficients=coefficients, rebuild=rebuild, z_total=z_total,
                  z_mean=z_mean, outer=outer)
    for name, *where in SCHEDULE:
        events[name](*where)

    for cp in basis_out + basis_z + basis_on + basis_on_z + [basis_core]:
        cp.wait_send()

    own_end()

    done(s1.at[0], sb).wait()
    done(s2.at[0], ps).wait()
    done(s3.at[0], xs).wait()
    done(s5.at[0], pr).wait()
    for k in range(STAGES):
        for h in range(2):
            ysend(k, h).wait_send()
    done(zs.at[0], rz.at[:, :, pl.ds(1, 7)]).wait()
    done(as_.at[0], rz.at[:, :, pl.ds(1, 7)]).wait()
    done(osem.at[0], er.at[:, :, :, pl.ds(0, ROWS)]).wait()
    done(s6.at[0], sb).wait()
    done(r6.at[0], sb).wait()


def exchange_step(grads, errors, basis):
    K = STAGES
    any_, vmem = pl.BlockSpec(memory_space=pl.ANY), pl.BlockSpec(memory_space=pltpu.VMEM)
    hbm = pl.BlockSpec(memory_space=pltpu.HBM)
    D = pltpu.SemaphoreType.DMA
    V = pltpu.VMEM
    return pl.pallas_call(
        kernel,
        out_shape=(jax.ShapeDtypeStruct(grads.shape, BF16), jax.ShapeDtypeStruct((ROWS, 512), F32)),
        in_specs=[hbm, hbm, hbm],
        out_specs=(any_, vmem),
        scratch_shapes=[
            V((ROWS, 8192), BF16),
            V((ROWS, 8192), BF16),
            V((K, 2, 3, 2, ROWS, 256), BF16),
            V((K, 2, 2, 4 * ROWS, 256), BF16),
            V((11 * ROWS, RANK), BF16),
            V((RANK, 10 * ROWS), BF16),
            V((K, 2, RANK, 256), BF16),
            V((K, 2, RANK, 256), F32),
            V((K, 2, RANK, 256), BF16),
            V((K, 2, RANK, 256), BF16),
            V((K, 2, RANK, 256), BF16),
            V((K, 2, 2, RANK, 256), BF16),
            V((K, 2, 2, 4 * ROWS, 256), BF16),
            V((K, 2, 8, 64, LANES), BF16),
            V((K, 2, 8, 64, LANES), BF16),
            V((K, 2, 64, LANES), F32),
            V((K, 2, 64, LANES), F32),
            V((K, 2, 8, 64, LANES), BF16),
            D((4,)),
            D((16,)), D((15,)),
            D((1,)), D((K, 2, 2)),
            D((1,)), D((K, 2)),
            D((1,)), D((K, 2)),
            D((1,)), D((K, 2)),
            D((1,)), D((1,)),
            D((1,)), D((K, 2)),
            D((K, 2)), D((K, 2)),
            D((1,)), D((K, 2)),
            D((1,)),
            D((1,)),
        ],
        compiler_params=pltpu.CompilerParams(
            collective_id=0, has_side_effects=True, vmem_limit_bytes=40 << 20),
        name="exchange_step",
    )(*(pltpu.with_memory_space_constraint(a, pltpu.HBM) for a in (grads, errors, basis)))


def body(grads, errors, basis, params, momentum):
    new_error, outer_grad = exchange_step(grads, errors, basis)
    new_momentum = momentum_rate * momentum + outer_grad
    new_params = params - outer_rate * (outer_grad + momentum_rate * new_momentum)
    return (new_params, new_momentum, new_error)


def solution(mesh):
    in_specs = (
        P("replica", "shard", None),
        P("replica", "shard", None),
        P("shard", None),
        P("replica", "shard"),
        P("replica", "shard"),
    )
    out_specs = (P("replica", "shard"), P("replica", "shard"), P("replica", "shard", None))
    return jax.shard_map(body, mesh=mesh, in_specs=in_specs, out_specs=out_specs, check_vma=False)
```
